256 devices in a mesh: seg: 16 (over z, x_hi), tp: 8 (over y, core), dp: 2 (over x_lo).
Axes of the slice: x: 4 (x_hi: 2, x_lo: 2; x = x_hi * 2 + x_lo), y: 4, z: 8, core: 2. Of those that a mesh axis runs over, the one named last changes fastest.
Arguments:
- tokens: bfloat16 [32768, 4096], P(('dp', 'seg')), parts along dimension 0, may hold values from -64 to 64
- w_query: bfloat16 [4096, 2048], P(None, 'tp'), may hold values from -1 to 1
- w_key: bfloat16 [4096, 2048], P(None, 'tp'), may hold values from -1 to 1
- w_value: bfloat16 [4096, 2048], P(None, 'tp'), may hold values from -0.09375 to 0.09375
- w_out: bfloat16 [2048, 4096], P('tp'), may hold values from -1 to 1
- mem_gate: float32 [16], P('tp'), may hold values from -2 to 2
- resets: int32 [32], P(('dp', 'seg')), parts along dimension 0, may hold values 0 or 1
Outputs:
- layer_out: bfloat16 [32768, 4096], P(('dp', 'seg'), 'tp'), parts along dimension 0
The draws below stay inside these ranges and needn't reach their ends.
There are 2 independent parts, one for each index of `dp`. The reference program is written for one: setup_inputs(seed, part) draws one part's arguments, and reference() takes and returns one part's arrays. A program takes and returns all parts, laid end to end along the dimension named above; an argument that names none is the same for every part. Nothing has to cross between parts.
All inputs are finite; a program needn't handle non-finite values. No bound on the sum of `resets` on one device may be relied on, other than what follows from the above.
Results may differ from the reference program's by a relative error of at most 0.014.
Values may be sent and summed in bfloat16 or wider, within the bound.
No kernel may reach another device: no remote copies, remote signals or barrier semaphores. Data moves between devices by JAX's collectives and lax.ppermute only.
A program may use at most 128 MiB of HBM per device.

```python
import math
import jax
import jax.numpy as jnp
from jax import lax

D = 4096
HEADS = 16
DH = 128
SEG_LEN = 1024
SEQ = 16384
N_SEG = 16
N_TP = 8


def draw_tokens(key, part):
    key_rows = jax.random.fold_in(key, 21)
    key_base = jax.random.fold_in(key, 22)
    row_scale = jnp.exp(jax.random.uniform(key_rows, (SEQ, 1), jnp.float32, math.log(0.3), math.log(3.0)))
    result = jnp.clip(jax.random.normal(key_base, (SEQ, D), jnp.float32), -4.0, 4.0) * row_scale
    return result.astype(jnp.bfloat16)


def shared_query(key):
    raw = jnp.clip(jax.random.normal(jax.random.fold_in(key, 11), (D, HEADS * DH), jnp.float32), -6.0, 6.0)
    return raw * (0.5 / math.sqrt(D))


def draw_w_query(key, part):
    return shared_query(key).astype(jnp.bfloat16)


def draw_w_key(key, part):
    other = jnp.clip(jax.random.normal(jax.random.fold_in(key, 12), (D, HEADS * DH), jnp.float32), -6.0, 6.0) * (0.5 / math.sqrt(D))
    result = other
    return result.astype(jnp.bfloat16)


def place_ends(drawn, own_key, low, top_value):
    index_at = [jax.random.randint(jax.random.fold_in(own_key, axis), (), 0, length) for axis, length in enumerate(drawn.shape)]
    longest = drawn.shape.index(max(drawn.shape))
    next_to = index_at[:longest] + [(index_at[longest] + 1) % drawn.shape[longest]] + index_at[longest + 1:]
    return drawn.at[tuple(index_at)].set(low).at[tuple(next_to)].set(top_value)


def block_scale(rng, dims, cuts, low, high):
    gain = 1.0
    for axis_at, blocks in cuts:
        steps = jax.random.uniform(jax.random.fold_in(jax.random.fold_in(rng, 6), axis_at), (blocks,), jnp.float32, low / len(cuts), high / len(cuts))
        gain = gain * jnp.repeat(jnp.exp(steps), dims[axis_at] // blocks).reshape((-1,) + (1,) * (len(dims) - 1 - axis_at))
    return gain


def gaussian(own_key, extent, deviation, limit, split=(), kind=jnp.bfloat16):
    factor_of = block_scale(own_key, extent, split, -0.22, 0.18) if split else 1.0
    drawn = jax.random.normal(own_key, extent, jnp.float32) * deviation * factor_of
    return jnp.minimum(jnp.maximum(drawn, -limit), limit).astype(kind)


def setup_inputs(seed: int = 0, part: int = 0) -> dict:
    key_of = jax.random.split(jax.random.key(seed), 8)
    own_keys = jax.random.split(jax.random.fold_in(key_of[7], part), 8)
    return {
        "tokens": draw_tokens(jax.random.fold_in(jax.random.fold_in(key_of[7], part), 71), part),
        "w_query": draw_w_query(jax.random.fold_in(key_of[7], 71), part),
        "w_key": draw_w_key(jax.random.fold_in(key_of[7], 71), part),
        "w_value": gaussian(key_of[3], (D, HEADS * DH), D ** -0.5, 0.09375, ((1, 8),)),
        "w_out": gaussian(key_of[4], (HEADS * DH, D), (HEADS * DH // 64) ** -0.5, 1.0, ((0, 8),)),
        "mem_gate": jnp.clip(jax.random.uniform(key_of[5], (HEADS,), jnp.float32, -2.0, 2.0) * block_scale(key_of[5], (HEADS,), ((0, 8),), -0.4, 0.0), -2.0, 2.0),
        "resets": place_ends((jax.random.randint(own_keys[6], (N_SEG,), 0, 5) < 1).astype(jnp.int32), jax.random.fold_in(own_keys[6], 1), 0, 1),
    }


def features(field):
    return jnp.where(field > 0, field + 1.0, jnp.exp(jnp.minimum(field, 0.0)))

def reference(tokens, w_query, w_key, w_value, w_out, mem_gate, resets):

    def project(weight):
        whole = jnp.dot(tokens, weight, preferred_element_type=jnp.float32).astype(jnp.bfloat16)
        return whole.reshape(N_SEG, SEG_LEN, HEADS, DH)
    queries = project(w_query)
    keys_all = project(w_key)
    vals_all = project(w_value)
    query_feat = features(queries.astype(jnp.float32))
    key_feat = features(keys_all.astype(jnp.float32))
    delta_mem = jnp.einsum('sthd,sthe->shde', key_feat, vals_all.astype(jnp.float32), precision=lax.Precision.HIGHEST)
    delta_norm = lax.optimization_barrier(jnp.sum(key_feat, axis=1))
    keep = 1.0 - resets.astype(jnp.float32)

    def advance(carry, item):
        memory, normer = carry
        keep_one, dmem, dnorm = item
        read_mem = keep_one * memory
        read_norm = keep_one * normer
        return ((read_mem + dmem, read_norm + dnorm), (read_mem, read_norm))
    start_state = (jnp.zeros((HEADS, DH, DH), jnp.float32), jnp.zeros((HEADS, DH), jnp.float32))
    _, (read_mem, read_norm) = lax.scan(advance, start_state, (keep, delta_mem, delta_norm))
    numer = jnp.einsum('sthd,shde->sthe', query_feat, read_mem, precision=lax.Precision.HIGHEST)
    denom = jnp.maximum(jnp.einsum('sthd,shd->sth', query_feat, read_norm, precision=lax.Precision.HIGHEST), 1.0)
    mem_att = numer / denom[..., None]

    def local_block(block):
        block_q, block_k, block_v = block
        scores = jnp.einsum('thd,uhd->htu', block_q.astype(jnp.float32), block_k.astype(jnp.float32), precision=lax.Precision.HIGHEST) / math.sqrt(DH)
        rows_idx = lax.broadcasted_iota(jnp.int32, (SEG_LEN, SEG_LEN), 0)
        cols_idx = lax.broadcasted_iota(jnp.int32, (SEG_LEN, SEG_LEN), 1)
        scores = jnp.where((rows_idx >= cols_idx)[None], scores, -1e+30)
        peak = lax.optimization_barrier(jnp.max(scores, axis=-1, keepdims=True))
        expo = jnp.exp(scores - peak)
        probs = (expo / lax.optimization_barrier(jnp.sum(expo, axis=-1, keepdims=True))).astype(jnp.bfloat16)
        return jnp.einsum('htu,uhd->thd', probs.astype(jnp.float32), block_v.astype(jnp.float32), precision=lax.Precision.HIGHEST)
    local_att = lax.map(local_block, (queries, keys_all, vals_all))
    gate = jax.nn.sigmoid(mem_gate)[None, None, :, None]
    attn = (gate * mem_att + (1.0 - gate) * local_att).astype(jnp.bfloat16).reshape(SEQ, HEADS * DH)
    group_cols = HEADS * DH // N_TP

    def add_group(total, group):
        start = (group * group_cols).astype(jnp.int32)
        cols = lax.dynamic_slice_in_dim(attn, start, group_cols, 1)
        rows = lax.dynamic_slice_in_dim(w_out, start, group_cols, 0)
        partial_value = jnp.dot(cols, rows, preferred_element_type=jnp.float32).astype(jnp.bfloat16)
        partial_value = lax.optimization_barrier(partial_value)
        return (total + partial_value.astype(jnp.float32), None)
    total, _ = lax.scan(add_group, jnp.zeros((SEQ, D), jnp.float32), jnp.arange(N_TP, dtype=jnp.int32))
    return total.astype(jnp.bfloat16)
```

```python
import math

import jax
import jax.numpy as jnp
from jax import lax
from jax.experimental import pallas as pl
from jax.experimental.pallas import tpu as pltpu
from jax.sharding import PartitionSpec as P

DH = 128
ROWS = DH + 8
BF = jnp.bfloat16
F32 = jnp.float32


def features(field):
    return jnp.where(field > 0, field + 1.0, jnp.exp(jnp.minimum(field, 0.0)))


def dot(a, b, dims=((1,), (0,))):
    return lax.dot_general(a, b, (dims, ((), ())), preferred_element_type=F32)


def call(kernel, out_shape, flops, moved, exps=0, **kw):
    return pl.pallas_call(
        kernel,
        out_shape=out_shape,
        cost_estimate=pl.CostEstimate(flops=flops, bytes_accessed=moved, transcendentals=exps),
        **kw,
    )


def kv_kernel(keep_ref, x_ref, wk_ref, wv_ref, k_ref, v_ref, s_ref, acc_ref):
    step = pl.program_id(0)
    last = pl.num_programs(0) - 1
    cols = wk_ref.shape[1]
    heads = cols // DH
    x = x_ref[...]

    @pl.when(step == 0)
    def _():
        acc_ref[:, :cols] = dot(x, wk_ref[...])
        acc_ref[:, cols:] = dot(x, wv_ref[...])

    @pl.when(step > 0)
    def _():
        acc_ref[:, :cols] += dot(x, wk_ref[...])
        acc_ref[:, cols:] += dot(x, wv_ref[...])

    @pl.when(step == last)
    def _():
        keys = acc_ref[:, :cols].astype(BF)
        vals = acc_ref[:, cols:].astype(BF)
        k_ref[...] = keys
        v_ref[...] = vals
        feat = features(keys.astype(F32))
        norm = jnp.sum(feat, axis=0, keepdims=True)
        feat_bf = feat.astype(BF)
        row = lax.broadcasted_iota(jnp.int32, (8, DH), 0)
        for h in range(heads):
            at = slice(h * DH, (h + 1) * DH)
            s_ref[h, :DH, :] = dot(vals[:, at], feat_bf[:, at], ((0,), (0,)))
            s_ref[h, DH:, :] = jnp.where(row == 0, norm[:, at], keep_ref[0])


def q_kernel(x_ref, w_ref, q_ref, f_ref, acc_ref):
    step = pl.program_id(0)
    last = pl.num_programs(0) - 1

    @pl.when(step == 0)
    def _():
        acc_ref[...] = dot(x_ref[...], w_ref[...])

    @pl.when(step > 0)
    def _():
        acc_ref[...] += dot(x_ref[...], w_ref[...])

    @pl.when(step == last)
    def _():
        queries = acc_ref[...].astype(BF)
        q_ref[...] = queries
        f_ref[...] = features(queries.astype(F32)).astype(BF)


def attend_kernel(q_ref, k_ref, v_ref, o_ref):
    toks = q_ref.shape[0]
    tile = 256
    scale = math.log2(math.e) / math.sqrt(DH)
    row = lax.broadcasted_iota(jnp.int32, (tile, tile), 0)
    col = lax.broadcasted_iota(jnp.int32, (tile, tile), 1)
    for i in range(toks // tile):
        at = slice(i * tile, (i + 1) * tile)
        q = q_ref[at, :]
        diag = jnp.where(row >= col, dot(q, k_ref[at, :], ((1,), (1,))), -1e30)
        peak = jnp.max(diag, axis=-1, keepdims=True)
        if i:
            past = dot(q, k_ref[: i * tile, :], ((1,), (1,)))
            peak = jnp.maximum(peak, jnp.max(past, axis=-1, keepdims=True))
        e = jnp.exp2((diag - peak) * scale)
        total = jnp.sum(e, axis=-1, keepdims=True)
        out = dot(e.astype(BF), v_ref[at, :])
        if i:
            e = jnp.exp2((past - peak) * scale)
            total = total + jnp.sum(e, axis=-1, keepdims=True)
            out = out + dot(e.astype(BF), v_ref[: i * tile, :])
        o_ref[at, :] = out / total


def read_kernel(gate_ref, f_ref, s_ref, *rest):
    local_refs, o_ref = rest[:-1], rest[-1]
    for h, l_ref in enumerate(local_refs):
        at = slice(h * DH, (h + 1) * DH)
        got = dot(f_ref[:, at], s_ref[h].astype(BF), ((1,), (1,)))
        gate = gate_ref[h]
        part = gate / jnp.maximum(got[:, DH : DH + 1], 1.0)
        o_ref[:, at] = (got[:, :DH] * part + (1.0 - gate) * l_ref[...]).astype(BF)


def rows_of(w_ref, block, depth):
    return w_ref[pl.ds(pl.multiple_of(block * depth, depth), depth), :]


def first_kernel(at_ref, a_ref, b_ref, c_ref, w_ref, o_ref):
    depth = a_ref.shape[1]
    o_ref[0] = (
        dot(a_ref[...], rows_of(w_ref, at_ref[1], depth))
        + dot(b_ref[...], rows_of(w_ref, at_ref[2], depth))
        + dot(c_ref[...], rows_of(w_ref, at_ref[3], depth))
    )


def last_kernel(at_ref, up_ref, down_ref, w_ref, acc_ref, o_ref):
    half, depth = up_ref.shape
    w = rows_of(w_ref, at_ref[4], depth)
    o_ref[:half, :] = (acc_ref[0, :half, :] + dot(up_ref[...], w)).astype(o_ref.dtype)
    o_ref[half:, :] = (acc_ref[0, half:, :] + dot(down_ref[...], w)).astype(o_ref.dtype)


def compose(low_a, low_d, high_a, high_d):
    return low_a * high_a, high_a * low_d + high_d


def on_device(tokens, w_query, w_key, w_value, w_out, mem_gate, resets):
    toks, width = tokens.shape
    cols = w_query.shape[1]
    heads = cols // DH
    n_tp = lax.axis_size("tp")
    n_seg = lax.axis_size("seg")
    n_y = n_tp // 2
    tp = lax.axis_index("tp")
    seg = lax.axis_index("seg")
    out_cols = w_out.shape[1] // n_tp
    chunk = 512
    steps = width // chunk

    keep = 1.0 - resets.astype(F32)
    gate = jax.nn.sigmoid(mem_gate)
    y, core = tp // 2, tp % 2
    where = jnp.stack([core, y, (y + n_y - 1) % n_y, (y + 1) % n_y, (y + 2) % n_y]).astype(jnp.int32)

    smem = pl.BlockSpec(memory_space=pltpu.SMEM)
    whole = pl.BlockSpec(memory_space=pltpu.VMEM)

    keys, vals, state = call(
        kv_kernel,
        (
            jax.ShapeDtypeStruct((toks, cols), BF),
            jax.ShapeDtypeStruct((toks, cols), BF),
            jax.ShapeDtypeStruct((heads, ROWS, DH), F32),
        ),
        4 * toks * width * cols,
        2 * (toks * width + 2 * width * cols + 2 * toks * cols),
        grid=(steps,),
        in_specs=[
            smem,
            pl.BlockSpec((toks, chunk), lambda i: (0, i)),
            pl.BlockSpec((chunk, cols), lambda i: (i, 0)),
            pl.BlockSpec((chunk, cols), lambda i: (i, 0)),
        ],
        out_specs=(
            pl.BlockSpec((toks, cols), lambda i: (0, 0)),
            pl.BlockSpec((toks, cols), lambda i: (0, 0)),
            pl.BlockSpec((heads, ROWS, DH), lambda i: (0, 0, 0)),
        ),
        scratch_shapes=[pltpu.VMEM((toks, 2 * cols), F32)],
        name="kv",
    )(keep, tokens, w_key, w_value)

    queries, q_feat = call(
        q_kernel,
        (jax.ShapeDtypeStruct((toks, cols), BF), jax.ShapeDtypeStruct((toks, cols), BF)),
        2 * toks * width * cols,
        2 * (toks * width + width * cols + 2 * toks * cols),
        grid=(steps,),
        in_specs=[
            pl.BlockSpec((toks, chunk), lambda i: (0, i)),
            pl.BlockSpec((chunk, cols), lambda i: (i, 0)),
        ],
        out_specs=(
            pl.BlockSpec((toks, cols), lambda i: (0, 0)),
            pl.BlockSpec((toks, cols), lambda i: (0, 0)),
        ),
        scratch_shapes=[pltpu.VMEM((toks, cols), F32)],
        name="query",
    )(tokens, w_query)

    def attend(h):
        spec = pl.BlockSpec((toks, DH), lambda i: (0, h))
        return call(
            attend_kernel,
            jax.ShapeDtypeStruct((toks, DH), F32),
            4 * toks * toks * DH,
            10 * toks * DH,
            toks * toks,
            grid=(1,),
            in_specs=[spec] * 3,
            out_specs=pl.BlockSpec((toks, DH), lambda i: (0, 0)),
            name="attend",
        )(queries, keys, vals)

    local = [attend(h) for h in range(heads)]

    groups = [[i for i in range(n_tp) if i % 2 == c] for c in range(2)]
    w_mine = lax.all_to_all(w_out, "tp", 1, 0, axis_index_groups=groups, tiled=True)

    total_d, total_a = state, state[:, DH + 1 : DH + 2, :]
    before_d, before_a = jnp.zeros_like(state), jnp.ones_like(total_a)
    own_a = total_a
    bit = 1
    while bit < n_seg:
        pairs = [(i, i ^ bit) for i in range(n_seg)]
        got = lax.ppermute(
            jnp.concatenate([total_d[:, : DH + 1], jnp.broadcast_to(total_a, (heads, 7, DH))], 1).astype(BF),
            "seg",
            pairs,
        ).astype(F32)
        got_a = got[:, DH + 1 : DH + 2, :]
        upper = (seg & bit) != 0
        new_a, new_d = compose(got_a, got, before_a, before_d)
        before_a = jnp.where(upper, new_a, before_a)
        before_d = jnp.where(upper, new_d, before_d)
        total_d = jnp.where(upper, total_a * got + total_d, got_a * total_d + got)
        total_a = total_a * got_a
        bit *= 2
    read = own_a * before_d

    attn = call(
        read_kernel,
        jax.ShapeDtypeStruct((toks, cols), BF),
        4 * toks * DH * cols,
        8 * toks * cols,
        in_specs=[smem, whole, whole] + [whole] * heads,
        out_specs=whole,
        name="read",
    )(gate, q_feat, read, *local)

    def along(value, by):
        return lax.ppermute(value, "tp", [(i, (i + 2 * by) % n_tp) for i in range(n_tp)])

    below, above = along(attn, 1), along(attn, -1)
    half = toks // 2
    far_up, far_down = along(below[:half], 1), along(above[half:], -1)

    acc = call(
        first_kernel,
        jax.ShapeDtypeStruct((2, toks, out_cols), F32),
        6 * toks * cols * 2 * out_cols,
        8 * toks * out_cols + 8 * toks * cols,
        grid_spec=pltpu.PrefetchScalarGridSpec(
            num_scalar_prefetch=1,
            grid=(2,),
            in_specs=[pl.BlockSpec((toks, cols), lambda j, at: (0, 0))] * 3
            + [pl.BlockSpec((n_y * cols, out_cols), lambda j, at: (0, j + at[0] - 2 * j * at[0]))],
            out_specs=pl.BlockSpec((1, toks, out_cols), lambda j, at: (j, 0, 0)),
        ),
        name="first",
    )(where, attn, below, above, w_mine)

    def finish(j, dtype):
        return call(
            last_kernel,
            jax.ShapeDtypeStruct((toks, out_cols), dtype),
            2 * toks * cols * out_cols,
            6 * toks * out_cols,
            grid_spec=pltpu.PrefetchScalarGridSpec(
                num_scalar_prefetch=1,
                grid=(1,),
                in_specs=[pl.BlockSpec((half, cols), lambda i, at: (0, 0))] * 2
                + [
                    pl.BlockSpec((n_y * cols, out_cols), lambda i, at: (0, j + at[0] - 2 * j * at[0])),
                    pl.BlockSpec((1, toks, out_cols), lambda i, at: (j, 0, 0)),
                ],
                out_specs=pl.BlockSpec((toks, out_cols), lambda i, at: (0, 0)),
            ),
            name="finish",
        )(where, far_up, far_down, w_mine, acc)

    own = finish(0, F32)
    given = finish(1, BF)
    taken = lax.ppermute(given, "tp", [(i, i ^ 1) for i in range(n_tp)])
    return (own + taken.astype(F32)).astype(BF)


def solution(mesh):
    placed = (
        P(("dp", "seg"), None),
        P(None, "tp"),
        P(None, "tp"),
        P(None, "tp"),
        P("tp", None),
        P("tp"),
        P(("dp", "seg")),
    )
    return jax.shard_map(
        on_device, mesh=mesh, in_specs=placed, out_specs=P(("dp", "seg"), "tp"), check_vma=False
    )
```

```python
import functools
import math

import jax
import jax.numpy as jnp
from jax import lax
from jax.experimental import pallas as pl
from jax.experimental.pallas import tpu as pltpu
from jax.sharding import PartitionSpec as P


DH = 128
ROWS = DH + 8
BF = jnp.bfloat16
F32 = jnp.float32
MIB = 1 << 20


def features(field):
    return jnp.where(field > 0, field + 1.0, jnp.exp(jnp.minimum(field, 0.0)))


def stay(value):
    return pltpu.with_memory_space_constraint(value, pltpu.HBM)


def dot(a, b, dims=((1,), (0,))):
    return lax.dot_general(a, b, (dims, ((), ())), preferred_element_type=F32)


def call(kernel, out_shape, vmem, flops, moved, exps=0, **kw):
    return pl.pallas_call(
        kernel,
        out_shape=out_shape,
        cost_estimate=pl.CostEstimate(flops=flops, bytes_accessed=moved, transcendentals=exps),
        compiler_params=pltpu.CompilerParams(vmem_limit_bytes=vmem * MIB),
        **kw,
    )


def qkv_kernel(cuts, dp_ref, resets_ref, x_hbm, wq_hbm, wk_hbm, wv_hbm, wo_hbm, q_ref, k_ref, v_ref, s_ref, o_hbm, x_ref, w_ref, acc_ref, o_ref, sem, in_sem, out_sem):
    toks, cols = q_ref.shape
    heads = cols // DH
    copies = []
    for i, (lo, hi) in enumerate(cuts):
        at = slice(lo, hi)
        batch = [pltpu.make_async_copy(x_hbm.at[:, at], x_ref.at[:, at], sem.at[i, 0])]
        for j, w_hbm in enumerate((wk_hbm, wv_hbm, wq_hbm)):
            to = slice(j * cols, (j + 1) * cols)
            batch.append(pltpu.make_async_copy(w_hbm.at[at, :], w_ref.at[at, to], sem.at[i, j + 1]))
        for copy in batch:
            copy.start()
        copies.append(batch)
    pieces, _, slim = o_ref.shape
    wide = wo_hbm.shape[1] // pieces
    packs = []
    for j in range(pieces):
        share = pl.ds(pl.multiple_of(j * wide + dp_ref[0] * slim, slim), slim)
        packs.append(pltpu.make_async_copy(wo_hbm.at[:, share], o_ref.at[j], in_sem.at[j]))
    for copy in packs:
        copy.start()
    part = toks // 8
    for i, (lo, hi) in enumerate(cuts):
        at = slice(lo, hi)
        for copy in copies[i]:
            copy.wait()
        for r in range(8):
            rows = slice(r * part, (r + 1) * part)
            piece = dot(x_ref[rows, at], w_ref[at, :])
            if i == 0:
                acc_ref[rows, :] = piece
            else:
                acc_ref[rows, :] += piece
    moves = [pltpu.make_async_copy(o_ref.at[j], o_hbm.at[j], out_sem.at[j]) for j in range(pieces)]
    for pack, move in zip(packs, moves):
        pack.wait()
        move.start()
    keys = acc_ref[:, :cols].astype(BF)
    vals = acc_ref[:, cols : 2 * cols].astype(BF)
    queries = acc_ref[:, 2 * cols :].astype(BF)
    k_ref[...] = keys
    v_ref[...] = vals
    q_ref[...] = queries
    feat = features(keys.astype(F32))
    norm = jnp.sum(feat, axis=0, keepdims=True)
    feat_bf = feat.astype(BF)
    row = lax.broadcasted_iota(jnp.int32, (8, DH), 0)
    keep = 1.0 - resets_ref[0].astype(F32)
    for h in range(heads):
        at = slice(h * DH, (h + 1) * DH)
        memory = dot(vals[:, at], feat_bf[:, at], ((0,), (0,)))
        tail = jnp.where(row == 0, norm[:, at], keep)
        s_ref[h] = jnp.concatenate([memory, tail], axis=0).astype(BF)
    for move in moves:
        move.wait()


def joined(bit, seg, got, before, flag):
    upper = jnp.where(jnp.bitwise_and(seg, bit) != 0, 1.0, 0.0)
    below = got * before[DH + 1 : DH + 2, :]
    after = jnp.where(flag, below, below + before)
    return upper * after + (1.0 - upper) * before


def merge_kernel(bit, seg_ref, total_ref, got_ref, *rest):
    old_ref, new_ref, before_ref = rest if len(rest) == 3 else (None,) + rest
    flag = lax.broadcasted_iota(jnp.int32, (ROWS, DH), 0) > DH
    upper = jnp.where(jnp.bitwise_and(seg_ref[0], bit) != 0, 1.0, 0.0)
    for h in range(total_ref.shape[0]):
        total, got = total_ref[h].astype(F32), got_ref[h].astype(F32)
        before = jnp.where(flag, 1.0, 0.0) if old_ref is None else old_ref[h]
        before_ref[h] = joined(bit, seg_ref[0], got, before, flag)
        mine, theirs = total[DH + 1 : DH + 2, :], got[DH + 1 : DH + 2, :]
        low_first = upper * (mine * got + total) + (1.0 - upper) * (theirs * total + got)
        new_ref[h] = jnp.where(flag, got * total, low_first).astype(BF)


def attend_kernel(q_ref, k_ref, v_ref, o_ref, wide_ref):
    toks = q_ref.shape[0]
    tile = 256
    scale = math.log2(math.e) / math.sqrt(DH)
    row = lax.broadcasted_iota(jnp.int32, (tile, tile), 0)
    col = lax.broadcasted_iota(jnp.int32, (tile, tile), 1)
    wide_ref[:, :DH] = v_ref[...]
    wide_ref[:, DH:] = jnp.ones((toks, DH), BF)
    for i in range(toks // tile):
        at = slice(i * tile, (i + 1) * tile)
        q = q_ref[at, :]
        diag = jnp.where(row >= col, dot(q, k_ref[at, :], ((1,), (1,))), -1e30)
        peak = jnp.max(diag, axis=-1, keepdims=True)
        if i:
            past = dot(q, k_ref[: i * tile, :], ((1,), (1,)))
            peak = jnp.maximum(peak, jnp.max(past, axis=-1, keepdims=True))
        out = dot(jnp.exp2((diag - peak) * scale).astype(BF), wide_ref[at, :])
        if i:
            out = out + dot(jnp.exp2((past - peak) * scale).astype(BF), wide_ref[: i * tile, :])
        o_ref[at, :] = out[:, :DH] / out[:, DH:]


def read_kernel(bit, seg_ref, resets_ref, gate_ref, q_ref, got_ref, before_ref, *rest):
    local_refs, top_ref, low_ref = rest[:-2], rest[-2], rest[-1]
    half = top_ref.shape[0]
    flag = lax.broadcasted_iota(jnp.int32, (ROWS, DH), 0) > DH
    keep = 1.0 - resets_ref[0].astype(F32)
    for h, l_ref in enumerate(local_refs):
        at = slice(h * DH, (h + 1) * DH)
        state = (keep * joined(bit, seg_ref[0], got_ref[h].astype(F32), before_ref[h], flag)).astype(BF)
        gate = 1.0 / (1.0 + jnp.exp(-jnp.full((1, DH), gate_ref[h], F32)))
        got = dot(features(q_ref[:, at].astype(F32)).astype(BF), state, ((1,), (1,)))
        part = gate[:, :1] / jnp.maximum(got[:, DH : DH + 1], 1.0)
        mixed = (got[:, :DH] * part + (1.0 - gate) * l_ref[...]).astype(BF)
        top_ref[:, at] = mixed[:half]
        low_ref[:, at] = mixed[half:]


def source(at_ref, shift, flip, size):
    j = jnp.bitwise_and(at_ref[0] + shift, size - 1)
    return jnp.bitwise_xor(j, 1) if flip else j


def project_kernel(plan, chained, reach, at_ref, w_hbm, *rest):
    values, rest = rest[: len(plan)], rest[len(plan) :]
    if chained:
        acc_ref, rest = rest[0], rest[1:]
    if reach:
        o_ref, far_ref, w_ref, sem, far_sem = rest
    else:
        o_ref, w_ref, sem = rest
    size = w_hbm.shape[0]
    half = values[0].shape[0]
    places = []
    for _, shift, flip in plan:
        if (shift, flip) not in places:
            places.append((shift, flip))
    copies = [
        pltpu.make_async_copy(w_hbm.at[source(at_ref, *where, size)], w_ref.at[i], sem.at[i])
        for i, where in enumerate(places)
    ]
    late = []
    if reach:
        late = [
            pltpu.make_async_copy(w_hbm.at[source(at_ref, 4, i == 1, size)], far_ref.at[i], far_sem.at[i])
            for i in range(2)
        ]
    for copy in copies + late:
        copy.start()
    for copy in copies:
        copy.wait()
    for side in range(2):
        rows = slice(side * half, (side + 1) * half)
        total = acc_ref[rows, :] if chained else None
        for value, (place, shift, flip) in zip(values, plan):
            if place == side:
                term = dot(value[...], w_ref[places.index((shift, flip))])
                total = term if total is None else total + term
        o_ref[rows, :] = total
    for copy in late:
        copy.wait()


def finish_kernel(dp_ref, mine_ref, twin_ref, acc_mine_ref, acc_twin_ref, top_ref, top_swap_ref, low_ref, low_swap_ref, o_ref):
    half = o_ref.shape[0]
    slim = mine_ref.shape[2]
    for side, parts in enumerate(((top_ref, top_swap_ref), (low_ref, low_swap_ref))):

        @pl.when(pl.program_id(0) == side)
        def _():
            rows = slice(side * half, (side + 1) * half)
            for index, w_ref, acc_ref in ((dp_ref[0], mine_ref, acc_mine_ref), (1 - dp_ref[0], twin_ref, acc_twin_ref)):
                total = acc_ref[rows, :]
                for i, part in enumerate(parts):
                    total = total + dot(part[...], w_ref[i])
                o_ref[:, pl.ds(pl.multiple_of(index * slim, slim), slim)] = total.astype(BF)


def on_device(tokens, w_query, w_key, w_value, w_out, mem_gate, resets):
    toks, width = tokens.shape
    cols = w_query.shape[1]
    heads = cols // DH
    half = toks // 2
    n_tp = lax.axis_size("tp")
    n_seg = lax.axis_size("seg")
    tp = lax.axis_index("tp")
    seg = lax.axis_index("seg")
    out_cols = w_out.shape[1] // n_tp

    n_dp = lax.axis_size("dp")
    twin = lax.axis_index("dp").astype(jnp.int32).reshape(1)
    place = tp.astype(jnp.int32).reshape(1)
    slim = out_cols // n_dp
    spot = seg.astype(jnp.int32).reshape(1)

    smem = pl.BlockSpec(memory_space=pltpu.SMEM)
    remote = pl.BlockSpec(memory_space=pltpu.HBM)
    whole = pl.BlockSpec(memory_space=pltpu.VMEM)

    edges = [0, 512, 1536, 2816, 4096]
    cuts = tuple(zip(edges[:-1], edges[1:]))
    flat = jax.ShapeDtypeStruct((toks, cols), BF)
    payload = jax.ShapeDtypeStruct((heads, ROWS, DH), BF)
    operands = (tokens, w_query, w_key, w_value, w_out)
    queries, keys, vals, state, w_cut = call(
        functools.partial(qkv_kernel, cuts),
        (flat, flat, flat, payload, jax.ShapeDtypeStruct((n_tp, cols, slim), BF)),
        36,
        6 * toks * width * cols,
        2 * (toks * width + 3 * width * cols + 4 * toks * cols),
        in_specs=[smem] * 2 + [remote] * 5,
        out_specs=(whole,) * 4 + (remote,),
        scratch_shapes=[
            pltpu.VMEM((toks, width), BF),
            pltpu.VMEM((width, 3 * cols), BF),
            pltpu.VMEM((toks, 3 * cols), F32),
            pltpu.VMEM((n_tp, cols, slim), BF),
            pltpu.SemaphoreType.DMA((len(cuts), 4)),
            pltpu.SemaphoreType.DMA((n_tp,)),
            pltpu.SemaphoreType.DMA((n_tp,)),
        ],
        name="qkv",
    )(twin, resets, *(stay(a) for a in operands))

    def attend(h):
        spec = pl.BlockSpec((toks, DH), lambda i: (0, h))
        return call(
            attend_kernel,
            jax.ShapeDtypeStruct((toks, DH), F32),
            10,
            4 * toks * toks * DH,
            10 * toks * DH,
            toks * toks,
            grid=(1,),
            in_specs=[spec] * 3,
            out_specs=pl.BlockSpec((toks, DH), lambda i: (0, 0)),
            scratch_shapes=[pltpu.VMEM((toks, 2 * DH), BF)],
            name="attend",
        )(queries, keys, vals)

    w_mine = stay(lax.all_to_all(stay(w_cut), "tp", 0, 0, tiled=True))
    w_twin = stay(lax.ppermute(w_mine, "dp", [(i, n_dp - 1 - i) for i in range(n_dp)]))

    local = []
    for h in range(heads):
        local.append(attend(h))

    total, before, bit, step = state, [], 1, 0
    while True:
        last = 2 * bit == n_seg
        if last:
            pairs = [(i, (n_seg // 2 - 1 - i // 2) * 2 + i % 2) for i in range(n_seg)]
        else:
            pairs = [(i, i ^ bit) for i in range(n_seg)]
        got = lax.ppermute(total, "seg", pairs)
        if last:
            break
        total, kept = call(
            functools.partial(merge_kernel, bit),
            (payload, jax.ShapeDtypeStruct(payload.shape, F32)),
            4,
            10 * heads * ROWS * DH,
            14 * heads * ROWS * DH,
            in_specs=[smem] + [whole] * (2 + len(before)),
            out_specs=(whole, whole),
            name="merge",
        )(spot, total, got, *before)
        before = [kept]
        bit *= 2
        step += 1

    row_half = jax.ShapeDtypeStruct((half, cols), BF)
    top, low = call(
        functools.partial(read_kernel, bit),
        (row_half, row_half),
        10,
        4 * toks * DH * cols,
        8 * toks * cols,
        in_specs=[smem] * 3 + [whole] * (3 + heads),
        out_specs=(whole, whole),
        name="read",
    )(spot, resets, mem_gate, queries, got, before[0], *local)

    def along(value, by):
        return lax.ppermute(value, "tp", [(i, (i + 2 * by) % n_tp) for i in range(n_tp)])

    def swap(value):
        return lax.ppermute(value, "tp", [(i, i ^ 1) for i in range(n_tp)])

    below_top, above_low = along(top, 1), along(low, -1)
    below_low, above_top = along(low, 1), along(top, -1)
    far_top, far_low = along(below_top, 1), along(above_low, -1)

    def pair(value, side, shift):
        return [(value, (side, shift, False)), (swap(value), (side, shift, True))]

    early = pair(top, 0, 0) + pair(low, 1, 0) + pair(below_top, 0, -2) + pair(above_low, 1, 2)
    second = pair(below_low, 1, -2) + pair(above_top, 0, 2)

    def project(parts, weights, acc, reach):
        values, plan = zip(*parts)
        places = len({where[1:] for where in plan})
        out = (jax.ShapeDtypeStruct((toks, slim), F32), jax.ShapeDtypeStruct((2, cols, slim), BF))
        return call(
            functools.partial(project_kernel, plan, acc is not None, reach),
            out if reach else out[0],
            14,
            2 * len(values) * half * cols * slim,
            2 * len(values) * half * cols + 6 * toks * slim,
            in_specs=[smem, remote] + [whole] * (len(values) + (acc is not None)),
            out_specs=(whole, whole) if reach else whole,
            scratch_shapes=[pltpu.VMEM((places, cols, slim), BF), pltpu.SemaphoreType.DMA((places,))]
            + [pltpu.SemaphoreType.DMA((2,))] * reach,
            name="project",
        )(place, weights, *values, *([] if acc is None else [acc]))

    acc_mine = project(early, w_mine, None, False)
    acc_mine, far_mine = project(second, w_mine, acc_mine, True)
    acc_twin, far_twin = project(early + second, w_twin, None, True)
    return call(
        finish_kernel,
        jax.ShapeDtypeStruct((toks, out_cols), BF),
        10,
        4 * toks * cols * out_cols,
        2 * toks * cols + 6 * toks * out_cols,
        grid=(2,),
        in_specs=[smem] + [whole] * 8,
        out_specs=pl.BlockSpec((half, out_cols), lambda i: (i, 0)),
        name="finish",
    )(twin, far_mine, far_twin, acc_mine, acc_twin, far_top, swap(far_top), far_low, swap(far_low))


def solution(mesh):
    placed = (
        P(("dp", "seg"), None),
        P(None, "tp"),
        P(None, "tp"),
        P(None, "tp"),
        P("tp", None),
        P("tp"),
        P(("dp", "seg")),
    )

    return jax.shard_map(on_device, mesh=mesh, in_specs=placed, out_specs=P(("dp", "seg"), "tp"), check_vma=False)
```

```python
import functools
import math

import jax
import jax.numpy as jnp
from jax import lax
from jax.experimental import pallas as pl
from jax.experimental.pallas import tpu as pltpu
from jax.sharding import PartitionSpec as P


DH = 128
ROWS = DH + 8
BF = jnp.bfloat16
F32 = jnp.float32
MIB = 1 << 20


def features(field):
    return jnp.where(field > 0, field + 1.0, jnp.exp(jnp.minimum(field, 0.0)))


def stay(value):
    return pltpu.with_memory_space_constraint(value, pltpu.HBM)


def dot(a, b, dims=((1,), (0,))):
    return lax.dot_general(a, b, (dims, ((), ())), preferred_element_type=F32)


def call(kernel, out_shape, vmem, flops, moved, exps=0, **kw):
    return pl.pallas_call(
        kernel,
        out_shape=out_shape,
        cost_estimate=pl.CostEstimate(flops=flops, bytes_accessed=moved, transcendentals=exps),
        compiler_params=pltpu.CompilerParams(vmem_limit_bytes=vmem * MIB),
        **kw,
    )


def qkv_kernel(cuts, dp_ref, resets_ref, x_hbm, wq_hbm, wk_hbm, wv_hbm, wo_hbm, q_ref, k_ref, v_ref, s_ref, o_hbm, x_ref, w_ref, acc_ref, o_ref, sem, in_sem, out_sem):
    toks, cols = q_ref.shape
    heads = cols // DH
    copies = []
    for i, (lo, hi) in enumerate(cuts):
        at = slice(lo, hi)
        batch = [pltpu.make_async_copy(x_hbm.at[:, at], x_ref.at[:, at], sem.at[i, 0])]
        for j, w_hbm in enumerate((wk_hbm, wv_hbm, wq_hbm)):
            to = slice(j * cols, (j + 1) * cols)
            batch.append(pltpu.make_async_copy(w_hbm.at[at, :], w_ref.at[at, to], sem.at[i, j + 1]))
        for copy in batch:
            copy.start()
        copies.append(batch)
    pieces, _, slim = o_ref.shape
    wide = wo_hbm.shape[1] // pieces
    packs = []
    for j in range(pieces):
        share = pl.ds(pl.multiple_of(j * wide + dp_ref[0] * slim, slim), slim)
        packs.append(pltpu.make_async_copy(wo_hbm.at[:, share], o_ref.at[j], in_sem.at[j]))
    for copy in packs:
        copy.start()
    moves = [pltpu.make_async_copy(o_ref.at[j], o_hbm.at[j], out_sem.at[j]) for j in range(pieces)]
    for i, (lo, hi) in enumerate(cuts[:-1]):
        at = slice(lo, hi)
        for copy in copies[i]:
            copy.wait()
        part = toks // 8
        for r in range(8):
            rows = slice(r * part, (r + 1) * part)
            piece = dot(x_ref[rows, at], w_ref[at, :])
            if i == 0:
                acc_ref[rows, :] = piece
            else:
                acc_ref[rows, :] += piece
    at = slice(*cuts[-1])
    for copy in copies[-1]:
        copy.wait()
    part = toks // 4
    norm, memory = None, [None] * heads
    for r in range(4):
        rows = slice(r * part, (r + 1) * part)
        whole = (acc_ref[rows, :] + dot(x_ref[rows, at], w_ref[at, :])).astype(BF)
        keys, vals = whole[:, :cols], whole[:, cols : 2 * cols]
        k_ref[rows, :] = keys
        v_ref[rows, :] = vals
        q_ref[rows, :] = whole[:, 2 * cols :]
        feat = features(keys.astype(F32))
        term = jnp.sum(feat, axis=0, keepdims=True)
        norm = term if norm is None else norm + term
        feat_bf = feat.astype(BF)
        for h in range(heads):
            of = slice(h * DH, (h + 1) * DH)
            term = dot(vals[:, of], feat_bf[:, of], ((0,), (0,)))
            memory[h] = term if memory[h] is None else memory[h] + term
        if r == 2:
            for pack, move in zip(packs, moves):
                pack.wait()
                move.start()
    row = lax.broadcasted_iota(jnp.int32, (8, DH), 0)
    keep = 1.0 - resets_ref[0].astype(F32)
    for h in range(heads):
        tail = jnp.where(row == 0, norm[:, h * DH : (h + 1) * DH], keep)
        s_ref[h] = jnp.concatenate([memory[h], tail], axis=0).astype(BF)
    for move in moves:
        move.wait()


def joined(bit, seg, got, before, flag):
    upper = jnp.where(jnp.bitwise_and(seg, bit) != 0, 1.0, 0.0)
    below = got * before[DH + 1 : DH + 2, :]
    after = jnp.where(flag, below, below + before)
    return upper * after + (1.0 - upper) * before


def merge_kernel(bit, seg_ref, total_ref, got_ref, *rest):
    old_ref, new_ref, before_ref = rest if len(rest) == 3 else (None,) + rest
    flag = lax.broadcasted_iota(jnp.int32, (ROWS, DH), 0) > DH
    upper = jnp.where(jnp.bitwise_and(seg_ref[0], bit) != 0, 1.0, 0.0)
    for h in range(total_ref.shape[0]):
        total, got = total_ref[h].astype(F32), got_ref[h].astype(F32)
        before = jnp.where(flag, 1.0, 0.0) if old_ref is None else old_ref[h]
        before_ref[h] = joined(bit, seg_ref[0], got, before, flag)
        mine, theirs = total[DH + 1 : DH + 2, :], got[DH + 1 : DH + 2, :]
        low_first = upper * (mine * got + total) + (1.0 - upper) * (theirs * total + got)
        new_ref[h] = jnp.where(flag, got * total, low_first).astype(BF)


def attend_kernel(head, gate_ref, q_ref, k_ref, v_ref, o_ref, f_ref, wide_ref):
    toks = q_ref.shape[0]
    tile = 256
    scale = math.log2(math.e) / math.sqrt(DH)
    row = lax.broadcasted_iota(jnp.int32, (tile, tile), 0)
    col = lax.broadcasted_iota(jnp.int32, (tile, tile), 1)
    other = 1.0 / (1.0 + jnp.exp(jnp.full((1, DH), gate_ref[head], F32)))
    wide_ref[:, :DH] = v_ref[...]
    wide_ref[:, DH:] = jnp.ones((toks, DH), BF)
    for i in range(toks // tile):
        at = slice(i * tile, (i + 1) * tile)
        q = q_ref[at, :]
        f_ref[at, :] = features(q.astype(F32)).astype(BF)
        diag = jnp.where(row >= col, dot(q, k_ref[at, :], ((1,), (1,))), -1e30)
        peak = jnp.max(diag, axis=-1, keepdims=True)
        if i:
            past = dot(q, k_ref[: i * tile, :], ((1,), (1,)))
            peak = jnp.maximum(peak, jnp.max(past, axis=-1, keepdims=True))
        out = dot(jnp.exp2((diag - peak) * scale).astype(BF), wide_ref[at, :])
        if i:
            out = out + dot(jnp.exp2((past - peak) * scale).astype(BF), wide_ref[: i * tile, :])
        o_ref[at, :] = (out[:, :DH] * (other / out[:, DH:])).astype(BF)


def read_kernel(bit, seg_ref, resets_ref, gate_ref, got_ref, before_ref, *rest):
    local_refs, top_ref, low_ref = rest[:-2], rest[-2], rest[-1]
    heads = len(local_refs) // 2
    half = top_ref.shape[0]
    flag = lax.broadcasted_iota(jnp.int32, (ROWS, DH), 0) > DH
    keep = 1.0 - resets_ref[0].astype(F32)
    for h, (l_ref, f_ref) in enumerate(zip(local_refs[:heads], local_refs[heads:])):
        at = slice(h * DH, (h + 1) * DH)
        state = (keep * joined(bit, seg_ref[0], got_ref[h].astype(F32), before_ref[h], flag)).astype(BF)
        gate = 1.0 / (1.0 + jnp.exp(-jnp.full((1, DH), gate_ref[h], F32)))
        got = dot(f_ref[...], state, ((1,), (1,)))
        part = gate[:, :1] / jnp.maximum(got[:, DH : DH + 1], 1.0)
        mixed = (got[:, :DH] * part + l_ref[...].astype(F32)).astype(BF)
        top_ref[:, at] = mixed[:half]
        low_ref[:, at] = mixed[half:]


def source(at_ref, shift, flip, size):
    j = jnp.bitwise_and(at_ref[0] + shift, size - 1)
    return jnp.bitwise_xor(j, 1) if flip else j


def project_kernel(plan, chained, reach, at_ref, w_hbm, *rest):
    values, rest = rest[: len(plan)], rest[len(plan) :]
    if chained:
        acc_ref, rest = rest[0], rest[1:]
    if reach:
        o_ref, far_ref, w_ref, sem, far_sem = rest
    else:
        o_ref, w_ref, sem = rest
    size = w_hbm.shape[0]
    half = values[0].shape[0]
    places = []
    for _, shift, flip in plan:
        if (shift, flip) not in places:
            places.append((shift, flip))
    copies = [
        pltpu.make_async_copy(w_hbm.at[source(at_ref, *where, size)], w_ref.at[i], sem.at[i])
        for i, where in enumerate(places)
    ]
    late = []
    if reach:
        late = [
            pltpu.make_async_copy(w_hbm.at[source(at_ref, 4, i == 1, size)], far_ref.at[i], far_sem.at[i])
            for i in range(2)
        ]
    for copy in copies + late:
        copy.start()
    for copy in copies:
        copy.wait()
    for side in range(2):
        rows = slice(side * half, (side + 1) * half)
        total = acc_ref[rows, :] if chained else None
        for value, (place, shift, flip) in zip(values, plan):
            if place == side:
                term = dot(value[...], w_ref[places.index((shift, flip))])
                total = term if total is None else total + term
        o_ref[rows, :] = total
    for copy in late:
        copy.wait()


def later_kernel(plan, at_ref, w_hbm, far_ref, acc_ref, *rest):
    values, (mine_ref, o_ref, last_ref, w_ref, sem, last_sem) = rest[: len(plan)], rest[len(plan) :]
    half = values[0].shape[0]
    last = pltpu.make_async_copy(w_hbm.at[source(at_ref, 4, True, w_hbm.shape[0])], last_ref, last_sem)
    last.start()
    project_kernel(plan, False, False, at_ref, w_hbm, *values, o_ref, w_ref, sem)
    for side, value in enumerate(values[-2:]):
        rows = slice(side * half, (side + 1) * half)
        mine_ref[rows, :] = acc_ref[rows, :] + dot(value[...], far_ref[0])
    last.wait()


def finish_kernel(dp_ref, mine_ref, twin_ref, acc_mine_ref, acc_twin_ref, top_ref, low_ref, o_ref):
    half, slim = o_ref.shape[0], twin_ref.shape[1]
    for side, part in enumerate((top_ref, low_ref)):

        @pl.when(pl.program_id(0) == side)
        def _():
            rows = slice(side * half, (side + 1) * half)
            mine = acc_mine_ref[rows, :] + dot(part[...], mine_ref[1])
            theirs = acc_twin_ref[rows, :] + dot(part[...], twin_ref[...])
            for index, total in ((dp_ref[0], mine), (1 - dp_ref[0], theirs)):
                o_ref[:, pl.ds(pl.multiple_of(index * slim, slim), slim)] = total.astype(BF)


def on_device(tokens, w_query, w_key, w_value, w_out, mem_gate, resets):
    toks, width = tokens.shape
    cols = w_query.shape[1]
    heads = cols // DH
    half = toks // 2
    n_tp = lax.axis_size("tp")
    n_seg = lax.axis_size("seg")
    tp = lax.axis_index("tp")
    seg = lax.axis_index("seg")
    out_cols = w_out.shape[1] // n_tp

    n_dp = lax.axis_size("dp")
    twin = lax.axis_index("dp").astype(jnp.int32).reshape(1)
    place = tp.astype(jnp.int32).reshape(1)
    slim = out_cols // n_dp
    spot = seg.astype(jnp.int32).reshape(1)

    smem = pl.BlockSpec(memory_space=pltpu.SMEM)
    remote = pl.BlockSpec(memory_space=pltpu.HBM)
    whole = pl.BlockSpec(memory_space=pltpu.VMEM)

    edges = [0, 512, 1536, 2816, 4096]
    cuts = tuple(zip(edges[:-1], edges[1:]))
    flat = jax.ShapeDtypeStruct((toks, cols), BF)
    payload = jax.ShapeDtypeStruct((heads, ROWS, DH), BF)
    operands = (tokens, w_query, w_key, w_value, w_out)
    queries, keys, vals, state, w_cut = call(
        functools.partial(qkv_kernel, cuts),
        (flat, flat, flat, payload, jax.ShapeDtypeStruct((n_tp, cols, slim), BF)),
        36,
        6 * toks * width * cols,
        2 * (toks * width + 3 * width * cols + 4 * toks * cols),
        in_specs=[smem] * 2 + [remote] * 5,
        out_specs=(whole,) * 4 + (remote,),
        scratch_shapes=[
            pltpu.VMEM((toks, width), BF),
            pltpu.VMEM((width, 3 * cols), BF),
            pltpu.VMEM((toks, 3 * cols), F32),
            pltpu.VMEM((n_tp, cols, slim), BF),
            pltpu.SemaphoreType.DMA((len(cuts), 4)),
            pltpu.SemaphoreType.DMA((n_tp,)),
            pltpu.SemaphoreType.DMA((n_tp,)),
        ],
        name="qkv",
    )(twin, resets, *(stay(a) for a in operands))

    def attend(h):
        spec = pl.BlockSpec((toks, DH), lambda i: (0, h))
        return call(
            functools.partial(attend_kernel, h),
            (jax.ShapeDtypeStruct((toks, DH), BF),) * 2,
            10,
            4 * toks * toks * DH,
            10 * toks * DH,
            toks * toks,
            grid=(1,),
            in_specs=[smem] + [spec] * 3,
            out_specs=(pl.BlockSpec((toks, DH), lambda i: (0, 0)),) * 2,
            scratch_shapes=[pltpu.VMEM((toks, 2 * DH), BF)],
            name="attend",
        )(mem_gate, queries, keys, vals)

    w_mine = stay(lax.all_to_all(stay(w_cut), "tp", 0, 0, tiled=True))
    w_twin = stay(lax.ppermute(w_mine, "dp", [(i, n_dp - 1 - i) for i in range(n_dp)]))

    local, q_feat = [], []
    for h in range(heads):
        got = attend(h)
        local.append(got[0])
        q_feat.append(got[1])

    total, before, bit, step = state, [], 1, 0
    while True:
        last = 2 * bit == n_seg
        if last:
            pairs = [(i, (n_seg // 2 - 1 - i // 2) * 2 + i % 2) for i in range(n_seg)]
        else:
            pairs = [(i, i ^ bit) for i in range(n_seg)]
        got = lax.ppermute(total, "seg", pairs)
        if last:
            break
        total, kept = call(
            functools.partial(merge_kernel, bit),
            (payload, jax.ShapeDtypeStruct(payload.shape, F32)),
            4,
            10 * heads * ROWS * DH,
            14 * heads * ROWS * DH,
            in_specs=[smem] + [whole] * (2 + len(before)),
            out_specs=(whole, whole),
            name="merge",
        )(spot, total, got, *before)
        before = [kept]
        bit *= 2
        step += 1

    row_half = jax.ShapeDtypeStruct((half, cols), BF)
    top, low = call(
        functools.partial(read_kernel, bit),
        (row_half, row_half),
        10,
        4 * toks * DH * cols,
        8 * toks * cols,
        in_specs=[smem] * 3 + [whole] * (2 + 2 * heads),
        out_specs=(whole, whole),
        name="read",
    )(spot, resets, mem_gate, got, before[0], *local, *q_feat)

    def along(value, by):
        return lax.ppermute(value, "tp", [(i, (i + 2 * by) % n_tp) for i in range(n_tp)])

    def swap(value):
        return lax.ppermute(value, "tp", [(i, i ^ 1) for i in range(n_tp)])

    below_top, above_low = along(top, 1), along(low, -1)
    below_low, above_top = along(low, 1), along(top, -1)
    far_top, far_low = along(below_top, 1), along(above_low, -1)

    def pair(value, side, shift):
        return [(value, (side, shift, False)), (swap(value), (side, shift, True))]

    early = pair(top, 0, 0) + pair(low, 1, 0) + pair(below_top, 0, -2) + pair(above_low, 1, 2)
    second = pair(below_low, 1, -2) + pair(above_top, 0, 2)

    def project(parts, weights, acc, reach):
        values, plan = zip(*parts)
        places = len({where[1:] for where in plan})
        out = (jax.ShapeDtypeStruct((toks, slim), F32), jax.ShapeDtypeStruct((2, cols, slim), BF))
        return call(
            functools.partial(project_kernel, plan, acc is not None, reach),
            out if reach else out[0],
            14,
            2 * len(values) * half * cols * slim,
            2 * len(values) * half * cols + 6 * toks * slim,
            in_specs=[smem, remote] + [whole] * (len(values) + (acc is not None)),
            out_specs=(whole, whole) if reach else whole,
            scratch_shapes=[pltpu.VMEM((places, cols, slim), BF), pltpu.SemaphoreType.DMA((places,))]
            + [pltpu.SemaphoreType.DMA((2,))] * reach,
            name="project",
        )(place, weights, *values, *([] if acc is None else [acc]))

    acc_mine = project(early, w_mine, None, False)
    acc_mine, far_mine = project(second, w_mine, acc_mine, True)
    ends = [(far_top, (0, 4, False)), (far_low, (1, 4, False))]
    far_swaps = (swap(far_top), swap(far_low))
    values, plan = zip(*(early + second + ends))
    places = len({where[1:] for where in plan})
    block = jax.ShapeDtypeStruct((toks, slim), F32)
    acc_mine, acc_twin, last_twin = call(
        functools.partial(later_kernel, plan),
        (block, block, jax.ShapeDtypeStruct((cols, slim), BF)),
        16,
        2 * (len(values) + 2) * half * cols * slim,
        2 * len(values) * half * cols + 10 * toks * slim,
        in_specs=[smem, remote] + [whole] * (2 + len(values)),
        out_specs=(whole,) * 3,
        scratch_shapes=[
            pltpu.VMEM((places, cols, slim), BF),
            pltpu.SemaphoreType.DMA((places,)),
            pltpu.SemaphoreType.DMA(()),
        ],
        name="later",
    )(place, w_twin, far_mine, acc_mine, *values)
    return call(
        finish_kernel,
        jax.ShapeDtypeStruct((toks, out_cols), BF),
        10,
        2 * toks * cols * out_cols,
        2 * toks * cols + 6 * toks * out_cols,
        grid=(2,),
        in_specs=[smem] + [whole] * 6,
        out_specs=pl.BlockSpec((half, out_cols), lambda i: (i, 0)),
        name="finish",
    )(twin, far_mine, last_twin, acc_mine, acc_twin, *far_swaps)


def solution(mesh):
    placed = (
        P(("dp", "seg"), None),
        P(None, "tp"),
        P(None, "tp"),
        P(None, "tp"),
        P("tp", None),
        P("tp"),
        P(("dp", "seg")),
    )

    return jax.shard_map(on_device, mesh=mesh, in_specs=placed, out_specs=P(("dp", "seg"), "tp"), check_vma=False)
```

```python
import functools
import math

import jax
import jax.numpy as jnp
from jax import lax
from jax.experimental import pallas as pl
from jax.experimental.pallas import tpu as pltpu
from jax.sharding import PartitionSpec as P


DH = 128
ROWS = DH + 8
BF = jnp.bfloat16
F32 = jnp.float32
MIB = 1 << 20


def features(field):
    return jnp.where(field > 0, field + 1.0, jnp.exp(jnp.minimum(field, 0.0)))


def stay(value):
    return pltpu.with_memory_space_constraint(value, pltpu.HBM)


def dot(a, b, dims=((1,), (0,))):
    return lax.dot_general(a, b, (dims, ((), ())), preferred_element_type=F32)


def call(kernel, out_shape, vmem, flops, moved, exps=0, **kw):
    return pl.pallas_call(
        kernel,
        out_shape=out_shape,
        cost_estimate=pl.CostEstimate(flops=flops, bytes_accessed=moved, transcendentals=exps),
        compiler_params=pltpu.CompilerParams(vmem_limit_bytes=vmem * MIB),
        **kw,
    )


def qkv_kernel(cuts, at_ref, dp_ref, resets_ref, x_hbm, wq_hbm, wk_hbm, wv_hbm, wo_hbm, q_ref, k_ref, v_ref, s_ref, o_hbm, own_ref, give_ref, x_ref, w_ref, wq_ref, acc_ref, o_ref, sem, q_sem, in_sem, out_sem, extra_sem):
    toks, cols = q_ref.shape
    heads = cols // DH
    copies = []
    for i, (lo, hi) in enumerate(cuts):
        at = slice(lo, hi)
        batch = [pltpu.make_async_copy(x_hbm.at[:, at], x_ref.at[:, at], sem.at[i, 0])]
        for j, w_hbm in enumerate((wk_hbm, wv_hbm)):
            to = slice(j * cols, (j + 1) * cols)
            batch.append(pltpu.make_async_copy(w_hbm.at[at, :], w_ref.at[at, to], sem.at[i, j + 1]))
        for copy in batch:
            copy.start()
        copies.append(batch)
    late = pltpu.make_async_copy(wq_hbm, wq_ref, q_sem)
    late.start()
    pieces, _, slim = o_ref.shape
    wide = wo_hbm.shape[1] // pieces
    packs, extras = [], []
    for j in range(pieces):
        share = pl.ds(pl.multiple_of(j * wide + dp_ref[0] * slim, slim), slim)
        packs.append(pltpu.make_async_copy(wo_hbm.at[:, share], o_ref.at[j], in_sem.at[j]))
    for i, to_ref in enumerate((own_ref, give_ref)):
        lo = jnp.bitwise_xor(at_ref[0], i) * wide + (1 - dp_ref[0]) * slim
        share = pl.ds(pl.multiple_of(lo, slim), slim)
        extras.append(pltpu.make_async_copy(wo_hbm.at[:, share], to_ref, extra_sem.at[i]))
    for copy in packs + extras:
        copy.start()
    moves = [pltpu.make_async_copy(o_ref.at[j], o_hbm.at[j], out_sem.at[j]) for j in range(pieces)]
    parts = 8
    part = toks // parts
    for i, (lo, hi) in enumerate(cuts):
        at = slice(lo, hi)
        for copy in copies[i]:
            copy.wait()
        for r in range(parts):
            rows = slice(r * part, (r + 1) * part)
            piece = dot(x_ref[rows, at], w_ref[at, :])
            if i > 0:
                piece = acc_ref[rows, :] + piece
            if i < len(cuts) - 1:
                acc_ref[rows, :] = piece
            else:
                whole = piece.astype(BF)
                k_ref[rows, :] = whole[:, :cols]
                v_ref[rows, :] = whole[:, cols:]
    late.wait()
    norm, memory = None, [None] * heads
    parts = 4
    part = toks // parts
    for r in range(parts):
        rows = slice(r * part, (r + 1) * part)
        q_ref[rows, :] = dot(x_ref[rows, :], wq_ref[...]).astype(BF)
        feat = features(k_ref[rows, :].astype(F32))
        term = jnp.sum(feat, axis=0, keepdims=True)
        norm = term if norm is None else norm + term
        feat_bf = feat.astype(BF)
        for h in range(heads):
            of = slice(h * DH, (h + 1) * DH)
            term = dot(v_ref[rows, of], feat_bf[:, of], ((0,), (0,)))
            memory[h] = term if memory[h] is None else memory[h] + term
        if r == 1:
            for pack, move in zip(packs, moves):
                pack.wait()
                move.start()
    row = lax.broadcasted_iota(jnp.int32, (8, DH), 0)
    keep = 1.0 - resets_ref[0].astype(F32)
    for h in range(heads):
        tail = jnp.where(row == 0, norm[:, h * DH : (h + 1) * DH], keep)
        s_ref[h] = jnp.concatenate([memory[h], tail], axis=0).astype(BF)
    for copy in moves + extras:
        copy.wait()


def joined(bit, seg, got, before, flag):
    upper = jnp.where(jnp.bitwise_and(seg, bit) != 0, 1.0, 0.0)
    below = got * before[DH + 1 : DH + 2, :]
    after = jnp.where(flag, below, below + before)
    return upper * after + (1.0 - upper) * before


def merge_kernel(bit, seg_ref, total_ref, got_ref, *rest):
    old_ref, new_ref, before_ref = rest if len(rest) == 3 else (None,) + rest
    flag = lax.broadcasted_iota(jnp.int32, (ROWS, DH), 0) > DH
    upper = jnp.where(jnp.bitwise_and(seg_ref[0], bit) != 0, 1.0, 0.0)
    for h in range(total_ref.shape[0]):
        total, got = total_ref[h].astype(F32), got_ref[h].astype(F32)
        before = jnp.where(flag, 1.0, 0.0) if old_ref is None else old_ref[h]
        before_ref[h] = joined(bit, seg_ref[0], got, before, flag)
        mine, theirs = total[DH + 1 : DH + 2, :], got[DH + 1 : DH + 2, :]
        low_first = upper * (mine * got + total) + (1.0 - upper) * (theirs * total + got)
        new_ref[h] = jnp.where(flag, got * total, low_first).astype(BF)


def attend_kernel(head, gate_ref, q_ref, k_ref, v_ref, o_ref, f_ref, wide_ref):
    toks = q_ref.shape[0]
    tile = 256
    scale = math.log2(math.e) / math.sqrt(DH)
    row = lax.broadcasted_iota(jnp.int32, (tile, tile), 0)
    col = lax.broadcasted_iota(jnp.int32, (tile, tile), 1)
    other = 1.0 / (1.0 + jnp.exp(jnp.full((1, DH), gate_ref[head], F32)))
    wide_ref[:, :DH] = v_ref[...]
    wide_ref[:, DH:] = jnp.ones((toks, DH), BF)
    for i in range(toks // tile):
        at = slice(i * tile, (i + 1) * tile)
        q = q_ref[at, :]
        f_ref[at, :] = features(q.astype(F32)).astype(BF)
        diag = jnp.where(row >= col, dot(q, k_ref[at, :], ((1,), (1,))), -1e30)
        peak = jnp.max(diag, axis=-1, keepdims=True)
        if i:
            past = dot(q, k_ref[: i * tile, :], ((1,), (1,)))
            peak = jnp.maximum(peak, jnp.max(past, axis=-1, keepdims=True))
        out = dot(jnp.exp2((diag - peak) * scale).astype(BF), wide_ref[at, :])
        if i:
            out = out + dot(jnp.exp2((past - peak) * scale).astype(BF), wide_ref[: i * tile, :])
        o_ref[at, :] = (out[:, :DH] * (other / out[:, DH:])).astype(BF)


def read_kernel(bit, seg_ref, resets_ref, gate_ref, got_ref, before_ref, *rest):
    local_refs, top_ref, low_ref = rest[:-2], rest[-2], rest[-1]
    heads = len(local_refs) // 2
    half = top_ref.shape[0]
    flag = lax.broadcasted_iota(jnp.int32, (ROWS, DH), 0) > DH
    keep = 1.0 - resets_ref[0].astype(F32)
    for h, (l_ref, f_ref) in enumerate(zip(local_refs[:heads], local_refs[heads:])):
        at = slice(h * DH, (h + 1) * DH)
        state = (keep * joined(bit, seg_ref[0], got_ref[h].astype(F32), before_ref[h], flag)).astype(BF)
        gate = 1.0 / (1.0 + jnp.exp(-jnp.full((1, DH), gate_ref[h], F32)))
        got = dot(f_ref[...], state, ((1,), (1,)))
        part = gate[:, :1] / jnp.maximum(got[:, DH : DH + 1], 1.0)
        mixed = (got[:, :DH] * part + l_ref[...].astype(F32)).astype(BF)
        top_ref[:, at] = mixed[:half]
        low_ref[:, at] = mixed[half:]


def pack_kernel(at_ref, mine_hbm, o_ref, near_ref, sem, near_sem):
    base = at_ref[0] - jnp.bitwise_and(at_ref[0], 1)
    size, skip = mine_hbm.shape[0], 2
    copies = []
    for r in range(skip, size):
        j = jnp.bitwise_and(base + r, size - 1)
        copies.append(pltpu.make_async_copy(mine_hbm.at[j], o_ref.at[r - skip], sem.at[r - skip]))
    for r in range(size):
        j = jnp.bitwise_and(base + r, size - 1)
        copies.append(pltpu.make_async_copy(mine_hbm.at[j], near_ref.at[r], near_sem.at[r]))
    for copy in copies:
        copy.start()
    for copy in copies:
        copy.wait()


def relative(at_ref, shift, flip):
    core = jnp.bitwise_and(at_ref[0], 1)
    return {0: 0, 2: 2, 4: 4, -2: 6}[shift] + (1 - core if flip else core)


def add_terms(plan, values, w_of, acc_ref, o_ref):
    half = values[0].shape[0]
    for side in range(2):
        rows = slice(side * half, (side + 1) * half)
        total = None if acc_ref is None else acc_ref[rows, :]
        for value, (place, shift, flip) in zip(values, plan):
            if place == side:
                term = dot(value[...], w_of(shift, flip))
                total = term if total is None else total + term
        o_ref[rows, :] = total


def near_kernel(plan, at_ref, w_ref, *rest):
    add_terms(plan, rest[:-1], lambda *where: w_ref[relative(at_ref, *where)], None, rest[-1])


def twin_block(at_ref, twin_ref, own_ref, part_ref, shift, flip):
    if shift == 0:
        return part_ref[...] if flip else own_ref[...]
    return twin_ref[relative(at_ref, shift, flip) - 2]


def middle_kernel(plan, skip, at_ref, w_ref, twin_ref, own_ref, part_ref, acc_ref, *rest):
    values, (mine_ref, o_ref) = rest[: len(plan)], rest[len(plan) :]
    add_terms(plan[skip:], values[skip:], lambda *where: w_ref[relative(at_ref, *where)], acc_ref, mine_ref)
    add_terms(plan, values, lambda *where: twin_block(at_ref, twin_ref, own_ref, part_ref, *where), None, o_ref)


def later_kernel(at_ref, w_ref, twin_ref, mine_in, twin_in, top_ref, low_ref, mine_ref, o_ref):
    half = top_ref.shape[0]
    j = relative(at_ref, 4, False)
    for side, value in enumerate((top_ref, low_ref)):
        rows = slice(side * half, (side + 1) * half)
        mine_ref[rows, :] = mine_in[rows, :] + dot(value[...], w_ref[j])
        o_ref[rows, :] = twin_in[rows, :] + dot(value[...], twin_ref[j - 2])


def finish_kernel(at_ref, dp_ref, mine_ref, twin_ref, acc_mine_ref, acc_twin_ref, top_ref, low_ref, o_ref):
    half, slim = o_ref.shape[0], twin_ref.shape[2]
    for side, part in enumerate((top_ref, low_ref)):

        @pl.when(pl.program_id(0) == side)
        def _():
            rows = slice(side * half, (side + 1) * half)
            mine = acc_mine_ref[rows, :] + dot(part[...], mine_ref[relative(at_ref, 4, True)])
            theirs = acc_twin_ref[rows, :] + dot(part[...], twin_ref[relative(at_ref, 4, True) - 2])
            for index, total in ((dp_ref[0], mine), (1 - dp_ref[0], theirs)):
                o_ref[:, pl.ds(pl.multiple_of(index * slim, slim), slim)] = total.astype(BF)


def on_device(tokens, w_query, w_key, w_value, w_out, mem_gate, resets):
    toks, width = tokens.shape
    cols = w_query.shape[1]
    heads = cols // DH
    half = toks // 2
    n_tp = lax.axis_size("tp")
    n_seg = lax.axis_size("seg")
    tp = lax.axis_index("tp")
    seg = lax.axis_index("seg")
    out_cols = w_out.shape[1] // n_tp

    n_dp = lax.axis_size("dp")
    twin = lax.axis_index("dp").astype(jnp.int32).reshape(1)
    place = tp.astype(jnp.int32).reshape(1)
    slim = out_cols // n_dp
    spot = seg.astype(jnp.int32).reshape(1)

    smem = pl.BlockSpec(memory_space=pltpu.SMEM)
    remote = pl.BlockSpec(memory_space=pltpu.HBM)
    whole = pl.BlockSpec(memory_space=pltpu.VMEM)

    edges = [0, 512, 1536, 2560, 3456, 4096]
    cuts = tuple(zip(edges[:-1], edges[1:]))
    flat = jax.ShapeDtypeStruct((toks, cols), BF)
    piece = jax.ShapeDtypeStruct((cols, slim), BF)
    payload = jax.ShapeDtypeStruct((heads, ROWS, DH), BF)
    operands = (tokens, w_query, w_key, w_value, w_out)
    queries, keys, vals, state, w_cut, w_own, w_give = call(
        functools.partial(qkv_kernel, cuts),
        (flat, flat, flat, payload, jax.ShapeDtypeStruct((n_tp, cols, slim), BF), piece, piece),
        36,
        6 * toks * width * cols,
        2 * (toks * width + 3 * width * cols + 4 * toks * cols),
        in_specs=[smem] * 3 + [remote] * 5,
        out_specs=(whole,) * 4 + (remote, whole, whole),
        scratch_shapes=[
            pltpu.VMEM((toks, width), BF),
            pltpu.VMEM((width, 2 * cols), BF),
            pltpu.VMEM((width, cols), BF),
            pltpu.VMEM((toks, 2 * cols), F32),
            pltpu.VMEM((n_tp, cols, slim), BF),
            pltpu.SemaphoreType.DMA((len(cuts), 3)),
            pltpu.SemaphoreType.DMA(()),
            pltpu.SemaphoreType.DMA((n_tp,)),
            pltpu.SemaphoreType.DMA((n_tp,)),
            pltpu.SemaphoreType.DMA((2,)),
        ],
        name="qkv",
    )(place, twin, resets, *(stay(a) for a in operands))

    def attend(h):
        spec = pl.BlockSpec((toks, DH), lambda i: (0, h))
        return call(
            functools.partial(attend_kernel, h),
            (jax.ShapeDtypeStruct((toks, DH), BF),) * 2,
            10,
            4 * toks * toks * DH,
            10 * toks * DH,
            toks * toks,
            grid=(1,),
            in_specs=[smem] + [spec] * 3,
            out_specs=(pl.BlockSpec((toks, DH), lambda i: (0, 0)),) * 2,
            scratch_shapes=[pltpu.VMEM((toks, 2 * DH), BF)],
            name="attend",
        )(mem_gate, queries, keys, vals)

    w_mine = stay(lax.all_to_all(stay(w_cut), "tp", 0, 0, tiled=True))
    others = jax.ShapeDtypeStruct((n_tp - 2, cols, slim), BF)
    w_send, w_near = call(
        pack_kernel,
        (others, jax.ShapeDtypeStruct((n_tp, cols, slim), BF)),
        8,
        0,
        4 * (2 * n_tp - 2) * cols * slim,
        in_specs=[smem, remote],
        out_specs=(whole, whole),
        scratch_shapes=[pltpu.SemaphoreType.DMA((n_tp - 2,)), pltpu.SemaphoreType.DMA((n_tp,))],
        name="pack",
    )(place, w_mine)
    w_twin = lax.ppermute(w_send, "dp", [(i, n_dp - 1 - i) for i in range(n_dp)])
    w_part = lax.ppermute(w_give, "tp", [(i, i ^ 1) for i in range(n_tp)])

    local, q_feat = [], []
    for h in range(heads):
        got = attend(h)
        local.append(got[0])
        q_feat.append(got[1])

    total, before, bit, step = state, [], 1, 0
    while True:
        last = 2 * bit == n_seg
        if last:
            pairs = [(i, (n_seg // 2 - 1 - i // 2) * 2 + i % 2) for i in range(n_seg)]
        else:
            pairs = [(i, i ^ bit) for i in range(n_seg)]
        got = lax.ppermute(total, "seg", pairs)
        if last:
            break
        total, kept = call(
            functools.partial(merge_kernel, bit),
            (payload, jax.ShapeDtypeStruct(payload.shape, F32)),
            4,
            10 * heads * ROWS * DH,
            14 * heads * ROWS * DH,
            in_specs=[smem] + [whole] * (2 + len(before)),
            out_specs=(whole, whole),
            name="merge",
        )(spot, total, got, *before)
        before = [kept]
        bit *= 2
        step += 1

    row_half = jax.ShapeDtypeStruct((half, cols), BF)
    top, low = call(
        functools.partial(read_kernel, bit),
        (row_half, row_half),
        10,
        4 * toks * DH * cols,
        8 * toks * cols,
        in_specs=[smem] * 3 + [whole] * (2 + 2 * heads),
        out_specs=(whole, whole),
        name="read",
    )(spot, resets, mem_gate, got, before[0], *local, *q_feat)

    def along(value, by):
        return lax.ppermute(value, "tp", [(i, (i + 2 * by) % n_tp) for i in range(n_tp)])

    def swap(value):
        return lax.ppermute(value, "tp", [(i, i ^ 1) for i in range(n_tp)])

    below_top, above_low = along(top, 1), along(low, -1)
    below_low, above_top = along(low, 1), along(top, -1)
    far_top, far_low = along(below_top, 1), along(above_low, -1)

    def pair(value, side, shift):
        return [(value, (side, shift, False)), (swap(value), (side, shift, True))]

    first = pair(below_top, 0, -2) + pair(above_low, 1, 2)
    early = pair(top, 0, 0) + pair(low, 1, 0) + first[::2]
    rest = first[1::2] + pair(below_low, 1, -2) + pair(above_top, 0, 2)
    far_swaps = (swap(far_top), swap(far_low))
    block = jax.ShapeDtypeStruct((toks, slim), F32)

    def project(kernel, name, shapes, terms, *operands):
        return call(
            kernel,
            shapes,
            16,
            2 * terms * half * cols * slim,
            2 * terms * half * cols + 8 * toks * slim,
            in_specs=[smem] + [whole] * (len(operands) - 1),
            out_specs=(whole,) * len(shapes),
            name=name,
        )(*operands)

    values, plan = zip(*early)
    (acc,) = project(functools.partial(near_kernel, plan), "near", (block,), len(plan), place, w_near, *values)
    values, plan = zip(*(early + rest))
    accs = project(
        functools.partial(middle_kernel, plan, len(early)), "middle", (block, block), len(plan) + len(rest),
        place, w_near, w_twin, w_own, w_part, acc, *values,
    )
    accs = project(later_kernel, "later", (block, block), 4, place, w_near, w_twin, *accs, far_top, far_low)
    return call(
        finish_kernel,
        jax.ShapeDtypeStruct((toks, out_cols), BF),
        10,
        2 * toks * cols * out_cols,
        2 * toks * cols + 6 * toks * out_cols,
        grid=(2,),
        in_specs=[smem] * 2 + [whole] * 6,
        out_specs=pl.BlockSpec((half, out_cols), lambda i: (i, 0)),
        name="finish",
    )(place, twin, w_near, w_twin, *accs, *far_swaps)


def solution(mesh):
    placed = (
        P(("dp", "seg"), None),
        P(None, "tp"),
        P(None, "tp"),
        P(None, "tp"),
        P("tp", None),
        P("tp"),
        P(("dp", "seg")),
    )

    return jax.shard_map(on_device, mesh=mesh, in_specs=placed, out_specs=P(("dp", "seg"), "tp"), check_vma=False)
```
